32 devices in a mesh: groups: 2 (over y), blk: 16 (over z, x, core).
Axes of the slice: x: 2, y: 2, z: 4, core: 2. Of those that a mesh axis runs over, the one named last changes fastest.
Arguments:
- txt_q: bfloat16 [1024, 1536], P(('groups', 'blk')), parts along dimension 0, may hold values from -40 to 40
- txt_k: bfloat16 [1024, 1536], P(('groups', 'blk')), parts along dimension 0, may hold values from -40 to 40
- txt_v: bfloat16 [1024, 1536], P(('groups', 'blk')), parts along dimension 0, may hold values from -6 to 6
- img_q: bfloat16 [2048, 1536], P(('groups', 'blk')), parts along dimension 0, may hold values from -6 to 6
- img_k: bfloat16 [2048, 1536], P(('groups', 'blk')), parts along dimension 0, may hold values from -6 to 6
- img_v: bfloat16 [2048, 1536], P(('groups', 'blk')), parts along dimension 0, may hold values from -6 to 6
- q_gain: float32 [128], replicated, may hold values from 0.35 to 3.5
- k_gain: float32 [128], replicated, may hold values from 0.35 to 3.5
- places: int32 [2048], P(('groups', 'blk')), parts along dimension 0, may hold values from 0 to 1023, each once
Outputs:
- txt_out: bfloat16 [1024, 1536], P(('groups', 'blk')), parts along dimension 0
- img_out: bfloat16 [2048, 1536], P(('groups', 'blk')), parts along dimension 0
The draws below stay inside these ranges and needn't reach their ends.
There are 2 independent parts, one for each index of `groups`. The reference program is written for one: setup_inputs(seed, part) draws one part's arguments, and reference() takes and returns one part's arrays. A program takes and returns all parts, laid end to end along the dimension named above; an argument that names none is the same for every part. Nothing has to cross between parts.
All inputs are finite; a program needn't handle non-finite values.
Results may differ from the reference program's by a relative error of at most 0.0055.
The reference program's roundings to bfloat16 on the way count: a program that leaves them out, or rounds other values in their place, can miss the bound.
Values may be sent and summed in bfloat16 or wider, within the bound.
No kernel may reach another device: no remote copies, remote signals or barrier semaphores. Data moves between devices by JAX's collectives and lax.ppermute only.
A program may use at most 64 MiB of HBM per device.

```python
import math
import jax
import jax.numpy as jnp
from jax import lax

HEADS = 12
HEAD_DIM = 128
TEXT = 512
GRID_W = 256
WIDTH = 1536
IMG = 1024


def text_pair(key):
    keys_drawn = jax.random.normal(jax.random.fold_in(key, 101), (TEXT, WIDTH), jnp.float32)
    queries_drawn = jax.random.normal(jax.random.fold_in(key, 102), (TEXT, WIDTH), jnp.float32)
    return (jnp.clip(queries_drawn, -40.0, 40.0), jnp.clip(keys_drawn, -40.0, 40.0))


def draw_txt_q(key, part):
    return text_pair(key)[0].astype(jnp.bfloat16)


def draw_txt_k(key, part):
    return text_pair(key)[1].astype(jnp.bfloat16)


def block_levels(stream_key, dims, shards, low, high):
    level, own = 1.0, jax.random.fold_in(stream_key, 6)
    for position, parts in shards:
        draws = jnp.exp(jax.random.uniform(jax.random.fold_in(own, position), (parts,), jnp.float32, low / len(shards), high / len(shards)))
        level = level * jnp.repeat(draws, dims[position] // parts).reshape([-1 if axis == position else 1 for axis in range(len(dims))])
    return level


def noise(key, extent, deviation, most, pieces=(), kind=jnp.bfloat16):
    loudness = block_levels(key, extent, pieces, -0.22, 0.18) if pieces else 1.0
    values = jax.random.normal(key, extent, jnp.float32) * deviation * loudness
    return jnp.minimum(jnp.maximum(values, -most), most).astype(kind)


def setup_inputs(seed: int = 0, part: int = 0) -> dict:
    key_list = jax.random.split(jax.random.key(seed), 10)
    part_keys = jax.random.split(jax.random.fold_in(key_list[9], part), 10)
    return {
        "txt_q": draw_txt_q(jax.random.fold_in(jax.random.fold_in(key_list[9], part), 71), part),
        "txt_k": draw_txt_k(jax.random.fold_in(jax.random.fold_in(key_list[9], part), 71), part),
        "txt_v": noise(part_keys[2], (TEXT, WIDTH), 1.0, 6.0, ((0, 16),)),
        "img_q": noise(part_keys[3], (IMG, WIDTH), 1.0, 6.0, ((0, 16),)),
        "img_k": noise(part_keys[4], (IMG, WIDTH), 1.0, 6.0, ((0, 16),)),
        "img_v": noise(part_keys[5], (IMG, WIDTH), 1.0, 6.0, ((0, 16),)),
        "q_gain": jnp.clip(jnp.exp(jax.random.uniform(key_list[6], (HEAD_DIM,), jnp.float32, math.log(0.35), math.log(3.5))), 0.35, 3.5),
        "k_gain": jnp.clip(jnp.exp(jax.random.uniform(key_list[7], (HEAD_DIM,), jnp.float32, math.log(0.35), math.log(3.5))), 0.35, 3.5),
        "places": jax.random.permutation(part_keys[8], IMG).astype(jnp.int32),
    }


rope_theta = 10000.0

def normed(values, gain):
    row_count = values.shape[0]
    heads = values.astype(jnp.float32).reshape(row_count, HEADS, HEAD_DIM)
    mean_sq = lax.optimization_barrier(jnp.mean(heads * heads, axis=-1, keepdims=True))
    return heads * lax.rsqrt(mean_sq + 1e-06) * gain

def rotate(heads, places):
    row_count = heads.shape[0]
    row_pos = (places // GRID_W).astype(jnp.float32)[:, None]
    col_pos = (places % GRID_W).astype(jnp.float32)[:, None]
    index = jnp.arange(64, dtype=jnp.float32)[None, :]
    freq_row = jnp.exp(-(index - 8.0) / 28.0 * jnp.log(rope_theta))
    freq_col = jnp.exp(-(index - 36.0) / 28.0 * jnp.log(rope_theta))
    angle = jnp.where(index < 8.0, 0.0 * row_pos, jnp.where(index < 36.0, row_pos * freq_row, col_pos * freq_col))
    cosine = jnp.cos(angle)[:, None, :]
    sine = jnp.sin(angle)[:, None, :]
    pairs = heads.reshape(row_count, HEADS, 64, 2)
    first = pairs[..., 0]
    second = pairs[..., 1]
    turned = jnp.stack([first * cosine - second * sine, first * sine + second * cosine], axis=-1)
    return turned.reshape(row_count, HEADS, HEAD_DIM)

def one_head(operands):
    queries, keys, values = operands
    row_count = queries.shape[0]
    block_size = 256 if row_count % 256 == 0 else row_count
    blocked = queries.reshape(row_count // block_size, block_size, HEAD_DIM)

    def one_block(query_block):
        scores = jnp.dot(query_block, keys.T, preferred_element_type=jnp.float32) / jnp.sqrt(jnp.float32(HEAD_DIM))
        top = lax.optimization_barrier(jnp.max(scores, axis=-1, keepdims=True))
        expo = jnp.exp(scores - top)
        total = lax.optimization_barrier(jnp.sum(expo, axis=-1, keepdims=True))
        mixed = jnp.dot(expo.astype(jnp.bfloat16), values, preferred_element_type=jnp.float32)
        return (mixed / total).astype(jnp.bfloat16)
    return lax.map(one_block, blocked).reshape(row_count, HEAD_DIM)

def reference(txt_q, txt_k, txt_v, img_q, img_k, img_v, q_gain, k_gain, places):
    queries = jnp.concatenate([normed(txt_q, q_gain).astype(jnp.bfloat16), rotate(normed(img_q, q_gain), places).astype(jnp.bfloat16)], axis=0)
    keys = jnp.concatenate([normed(txt_k, k_gain).astype(jnp.bfloat16), rotate(normed(img_k, k_gain), places).astype(jnp.bfloat16)], axis=0)
    values = jnp.concatenate([txt_v, img_v], axis=0)
    row_count = values.shape[0]
    values = values.reshape(row_count, HEADS, HEAD_DIM)
    result = lax.map(one_head, (jnp.transpose(queries, (1, 0, 2)), jnp.transpose(keys, (1, 0, 2)), jnp.transpose(values, (1, 0, 2))))
    result = jnp.transpose(result, (1, 0, 2)).reshape(row_count, HEADS * HEAD_DIM)
    return (result[:TEXT], result[TEXT:])
```

```python
import math
import jax
import jax.numpy as jnp
from jax import lax
from jax.experimental import pallas as pl
from jax.experimental.pallas import tpu as pltpu
from jax.sharding import PartitionSpec as P

HEADS = 12
HEAD_DIM = 128
GRID_W = 256


rope_theta = 10000.0


def from_partner(block, axis, apart):
    count = lax.axis_size(axis)
    route = []
    for low in range(count):
        high = low | 1 << apart
        if high != low and high < count:
            route += [(low, high), (high, low)]
    return lax.ppermute(block, axis, route)


def passed_along(block, axis, distance):
    devices = range(lax.axis_size(axis))
    route = [((i - distance) % len(devices), i) for i in devices]
    return lax.ppermute(block, axis, route)


def normed(values, gain):
    row_count = values.shape[0]
    heads = values.astype(jnp.float32).reshape(row_count, HEADS, HEAD_DIM)
    mean_sq = jnp.mean(heads * heads, axis=-1, keepdims=True)
    return heads * lax.rsqrt(mean_sq + 1e-06) * gain


def rotate(heads, places):
    row_count = heads.shape[0]
    row_pos = (places // GRID_W).astype(jnp.float32)[:, None]
    col_pos = (places % GRID_W).astype(jnp.float32)[:, None]
    index = jnp.arange(64, dtype=jnp.float32)[None, :]
    freq_row = jnp.exp(-(index - 8.0) / 28.0 * jnp.log(rope_theta))
    freq_col = jnp.exp(-(index - 36.0) / 28.0 * jnp.log(rope_theta))
    angle = jnp.where(
        index < 8.0, 0.0 * row_pos, jnp.where(index < 36.0, row_pos * freq_row, col_pos * freq_col)
    )
    cosine = jnp.cos(angle)[:, None, :]
    sine = jnp.sin(angle)[:, None, :]
    pairs = heads.reshape(row_count, HEADS, 64, 2)
    first = pairs[..., 0]
    second = pairs[..., 1]
    turned = jnp.stack([first * cosine - second * sine, first * sine + second * cosine], axis=-1)
    return turned.reshape(row_count, HEADS, HEAD_DIM)


def update(state_tuple, queries, pair_block):
    running_max, running_sum, running_acc = state_tuple
    key_block = pair_block[0]
    value_block = pair_block[1]
    scores = jnp.einsum("rhd,nhd->rhn", queries, key_block, preferred_element_type=jnp.float32)
    scores = scores / jnp.sqrt(jnp.float32(HEAD_DIM))
    new_max = jnp.maximum(running_max, jnp.max(scores, axis=-1))
    fade_out = jnp.exp(running_max - new_max)
    expo = jnp.exp(scores - new_max[..., None])
    new_sum = running_sum * fade_out + jnp.sum(expo, axis=-1)
    added = jnp.einsum(
        "rhn,nhd->rhd", expo.astype(jnp.bfloat16), value_block, preferred_element_type=jnp.float32
    )
    new_acc = running_acc * fade_out[..., None] + added
    return (new_max, new_sum, new_acc)


def regroup_swap(piece, bit_number):
    return from_partner(piece, "blk", bit_number)


def restore_swap(piece, bit_number):
    return from_partner(piece, "blk", bit_number)


def among_four(stacked, mover):
    index_here = lax.axis_index("blk")
    for bit_number in (0, 1):
        position = 1 - bit_number
        own_bit = index_here >> bit_number & 1
        kept_half = lax.dynamic_index_in_dim(stacked, own_bit, position, keepdims=False)
        sent_half = lax.dynamic_index_in_dim(stacked, 1 - own_bit, position, keepdims=False)
        received = mover(sent_half, bit_number)
        stacked = jnp.where(
            own_bit == 0,
            jnp.stack([kept_half, received], axis=position),
            jnp.stack([received, kept_half], axis=position),
        )
    return stacked


def move_upward(pair_block):
    return passed_along(pair_block, "blk", 4)


def move_downward(pair_block):
    return passed_along(pair_block, "blk", -4)


def per_device(txt_q, txt_k, txt_v, img_q, img_k, img_v, q_gain, k_gain, places):
    txt_count = txt_q.shape[0]
    img_count = img_q.shape[0]
    local_count = txt_count + img_count
    quarter = HEADS // 4
    queries = jnp.concatenate(
        [
            normed(txt_q, q_gain).astype(jnp.bfloat16),
            rotate(normed(img_q, q_gain), places).astype(jnp.bfloat16),
        ],
        axis=0,
    )
    keys_local = jnp.concatenate(
        [
            normed(txt_k, k_gain).astype(jnp.bfloat16),
            rotate(normed(img_k, k_gain), places).astype(jnp.bfloat16),
        ],
        axis=0,
    )
    values_local = jnp.concatenate([txt_v, img_v], axis=0).reshape(local_count, HEADS, HEAD_DIM)
    stacked = jnp.stack([queries, keys_local, values_local], axis=1).reshape(
        local_count, 3, 4, quarter, HEAD_DIM
    )
    stacked = jnp.transpose(stacked, (2, 0, 1, 3, 4)).reshape(
        2, 2, local_count, 3, quarter, HEAD_DIM
    )
    grouped = among_four(stacked, regroup_swap).reshape(4 * local_count, 3, quarter, HEAD_DIM)
    group_q = grouped[:, 0]
    own_pair = jnp.stack([grouped[:, 1], grouped[:, 2]], axis=0)
    group_rows = 4 * local_count
    blocks = lax.axis_size("blk") // 4
    soft_state = (
        jnp.full((group_rows, quarter), -jnp.inf, jnp.float32),
        jnp.zeros((group_rows, quarter), jnp.float32),
        jnp.zeros((group_rows, quarter, HEAD_DIM), jnp.float32),
    )
    soft_state = update(soft_state, group_q, own_pair)
    downward_turns = (blocks - 1) // 2

    def both_turn(turn, loop_state):
        upward, downward, inner = loop_state
        upward = move_upward(upward)
        downward = move_downward(downward)
        inner = update(inner, group_q, upward)
        inner = update(inner, group_q, downward)
        return (upward, downward, inner)

    upward, downward, soft_state = lax.fori_loop(
        0, downward_turns, both_turn, (own_pair, own_pair, soft_state)
    )
    upward = move_upward(upward)
    soft_state = update(soft_state, group_q, upward)
    running_max, running_sum, running_acc = soft_state
    result = (running_acc / running_sum[..., None]).astype(jnp.bfloat16)
    result = result.reshape(2, 2, local_count, quarter, HEAD_DIM)
    returned = among_four(result, restore_swap).reshape(4, local_count, quarter, HEAD_DIM)
    returned = jnp.transpose(returned, (1, 0, 2, 3)).reshape(local_count, HEADS * HEAD_DIM)
    return (returned[:txt_count], returned[txt_count:])


LANES_PER_HEAD = HEAD_DIM


def whole(count):
    return [pl.BlockSpec(memory_space=pltpu.VMEM)] * count


def unit_rows(x, gain):
    return x * lax.rsqrt(jnp.mean(x * x, axis=-1, keepdims=True) + 1e-06) * gain


def turn_tables(places_ref):
    count = places_ref.shape[1]
    spot = lax.broadcasted_iota(jnp.int32, (count, count), 0) == lax.broadcasted_iota(
        jnp.int32, (count, count), 1
    )
    patch = places_ref[...].astype(jnp.float32)
    patch = jnp.sum(jnp.where(spot, patch, 0.0), axis=1, keepdims=True)
    row_pos = jnp.floor(patch * (1.0 / GRID_W))
    col_pos = patch - row_pos * GRID_W
    lane = lax.broadcasted_iota(jnp.int32, (1, HEAD_DIM), 1)
    index = (lane >> 1).astype(jnp.float32)
    log_theta = jnp.float32(math.log(rope_theta))
    freq_row = jnp.exp(-(index - 8.0) / 28.0 * log_theta)
    freq_col = jnp.exp(-(index - 36.0) / 28.0 * log_theta)
    angle = jnp.where(
        index < 8.0, 0.0 * row_pos, jnp.where(index < 36.0, row_pos * freq_row, col_pos * freq_col)
    )
    even = (lane & 1) == 0
    sine = jnp.sin(angle)
    return jnp.cos(angle), jnp.where(even, -sine, sine), even


def turned(x, tables):
    cosine, sine, even = tables
    partner = jnp.where(even, pltpu.roll(x, HEAD_DIM - 1, 1), pltpu.roll(x, 1, 1))
    return x * cosine + partner * sine


def prepare(here_ref, places_ref, gain_ref, txt_ref, img_ref, out_refs, lead):
    tables = turn_tables(places_ref)
    gain = gain_ref[...]
    txt_count, width = txt_ref.shape
    share = width // len(out_refs)
    for slot, out_ref in enumerate(out_refs):
        base = (here_ref[0] ^ slot) * share
        for off in range(0, share, HEAD_DIM):
            cols = pl.ds(pl.multiple_of(base + off, HEAD_DIM), HEAD_DIM)
            txt = unit_rows(txt_ref[:, cols].astype(jnp.float32), gain)
            img = turned(unit_rows(img_ref[:, cols].astype(jnp.float32), gain), tables)
            out_ref[lead + (slice(0, txt_count), slice(off, off + HEAD_DIM))] = txt.astype(jnp.bfloat16)
            out_ref[lead + (slice(txt_count, None), slice(off, off + HEAD_DIM))] = img.astype(jnp.bfloat16)


def keys_kernel(here_ref, places_ref, gain_ref, txt_k, img_k, txt_v, img_v, *out_refs):
    prepare(here_ref, places_ref, gain_ref, txt_k, img_k, out_refs, (0,))
    txt_count, width = txt_v.shape
    share = width // len(out_refs)
    for slot, out_ref in enumerate(out_refs):
        cols = pl.ds(pl.multiple_of((here_ref[0] ^ slot) * share, HEAD_DIM), share)
        out_ref[1, :txt_count] = txt_v[:, cols]
        out_ref[1, txt_count:] = img_v[:, cols]


def queries_kernel(here_ref, places_ref, gain_ref, txt_q, img_q, *out_refs):
    prepare(here_ref, places_ref, gain_ref, txt_q, img_q, out_refs, ())


def stage_kernel(*refs):
    pieces, (key_ref, value_ref) = refs[:-2], refs[-2:]
    rows = pieces[0].shape[1]
    for i, piece in enumerate(pieces):
        key_ref[i * rows:(i + 1) * rows] = piece[0]
        value_ref[i * rows:(i + 1) * rows] = piece[1]


def attend_kernel(*refs):
    count = (len(refs) - 2) // 2
    query_refs, key_ref, value_ref, out_refs = refs[:count], refs[count], refs[count + 1], refs[count + 2:]
    rows, share = query_refs[0].shape
    scale = 1.0 / math.sqrt(HEAD_DIM)
    for off in range(0, share, HEAD_DIM):
        cols = slice(off, off + HEAD_DIM)
        q = jnp.concatenate([ref[:, cols] for ref in query_refs], axis=0)
        s = lax.dot_general(
            q, key_ref[:, cols], (((1,), (1,)), ((), ())), preferred_element_type=jnp.float32
        )
        top = jnp.max(s, axis=-1, keepdims=True)
        expo = jnp.exp((s - top) * scale)
        total = jnp.sum(expo, axis=-1, keepdims=True)
        mixed = jnp.dot(
            expo.astype(jnp.bfloat16), value_ref[:, cols], preferred_element_type=jnp.float32
        )
        result = (mixed / total).astype(jnp.bfloat16)
        for i, ref in enumerate(out_refs):
            ref[:, cols] = result[i * rows:(i + 1) * rows]


def gather_kernel(here_ref, *refs):
    pieces, (txt_ref, img_ref) = refs[:-2], refs[-2:]
    txt_count = txt_ref.shape[0]
    share = pieces[0].shape[1]
    for slot, piece in enumerate(pieces):
        cols = pl.ds(pl.multiple_of((here_ref[0] ^ slot) * share, HEAD_DIM), share)
        txt_ref[:, cols] = piece[:txt_count]
        img_ref[:, cols] = piece[txt_count:]


SMEM_SPEC = pl.BlockSpec(memory_space=pltpu.SMEM)


def to_partner(block, bits):
    count = lax.axis_size("blk")
    return lax.ppermute(block, "blk", [(i, i ^ bits) for i in range(count)])


def shape_of(*dims):
    return jax.ShapeDtypeStruct(dims, jnp.bfloat16)


def per_plane(txt_q, txt_k, txt_v, img_q, img_k, img_v, q_gain, k_gain, places):
    txt_count, width = txt_q.shape
    rows = txt_count + img_q.shape[0]
    share = width // 4
    here = (lax.axis_index("blk") >> 2).reshape(1)
    spots = places.reshape(1, -1)
    kv = pl.pallas_call(
        keys_kernel,
        out_shape=[shape_of(2, rows, share)] * 4,
        in_specs=[SMEM_SPEC] + whole(6),
        out_specs=whole(4),
        name="keys",
    )(here, spots, k_gain.reshape(1, -1), txt_k, img_k, txt_v, img_v)
    qs = pl.pallas_call(
        queries_kernel,
        out_shape=[shape_of(rows, share)] * 4,
        in_specs=[SMEM_SPEC] + whole(4),
        out_specs=whole(4),
        name="queries",
    )(here, spots, q_gain.reshape(1, -1), txt_q, img_q)
    own = [kv[0], None, None, None]
    q_in = [qs[0], None, None, None]
    for slot in (2, 3, 1):
        own[slot] = to_partner(kv[slot], slot << 2)
    for slot in (2, 3, 1):
        q_in[slot] = to_partner(qs[slot], slot << 2)
    pieces = []
    for slot in (0, 1, 2, 3):
        across = to_partner(own[slot], 2)
        pieces += [own[slot], across, to_partner(own[slot], 1), to_partner(across, 1)]
    keys, values = pl.pallas_call(
        stage_kernel,
        out_shape=[shape_of(len(pieces) * rows, share)] * 2,
        in_specs=whole(len(pieces)),
        out_specs=whole(2),
        name="stage",
    )(*pieces)

    def attend(a, b):
        return pl.pallas_call(
            attend_kernel,
            out_shape=[shape_of(rows, share)] * 2,
            in_specs=whole(4),
            out_specs=whole(2),
            name="attend",
        )(a, b, keys, values)

    far = attend(q_in[2], q_in[3])
    near = attend(q_in[0], q_in[1])
    back = [near[0], to_partner(near[1], 4), to_partner(far[0], 8), to_partner(far[1], 12)]
    return tuple(
        pl.pallas_call(
            gather_kernel,
            out_shape=[shape_of(txt_count, width), shape_of(rows - txt_count, width)],
            in_specs=[SMEM_SPEC] + whole(4),
            out_specs=whole(2),
            name="gather",
        )(here, *back)
    )


def solution(mesh):
    placed = (
        P(("groups", "blk"), None),
        P(("groups", "blk"), None),
        P(("groups", "blk"), None),
        P(("groups", "blk"), None),
        P(("groups", "blk"), None),
        P(("groups", "blk"), None),
        P(),
        P(),
        P(("groups", "blk")),
    )
    planes = mesh.shape["blk"] // 4
    return jax.shard_map(
        per_plane if planes == 4 else per_device,
        mesh=mesh,
        in_specs=placed,
        out_specs=(P(("groups", "blk"), None), P(("groups", "blk"), None)),
        check_vma=False,
    )
```

```python
import math
import jax
import jax.numpy as jnp
from jax import lax
from jax.experimental import pallas as pl
from jax.experimental.pallas import tpu as pltpu
from jax.sharding import PartitionSpec as P

HEADS = 12
HEAD_DIM = 128
GRID_W = 256


rope_theta = 10000.0


def from_partner(block, axis, apart):
    count = lax.axis_size(axis)
    route = []
    for low in range(count):
        high = low | 1 << apart
        if high != low and high < count:
            route += [(low, high), (high, low)]
    return lax.ppermute(block, axis, route)


def passed_along(block, axis, distance):
    devices = range(lax.axis_size(axis))
    route = [((i - distance) % len(devices), i) for i in devices]
    return lax.ppermute(block, axis, route)


def normed(values, gain):
    row_count = values.shape[0]
    heads = values.astype(jnp.float32).reshape(row_count, HEADS, HEAD_DIM)
    mean_sq = jnp.mean(heads * heads, axis=-1, keepdims=True)
    return heads * lax.rsqrt(mean_sq + 1e-06) * gain


def rotate(heads, places):
    row_count = heads.shape[0]
    row_pos = (places // GRID_W).astype(jnp.float32)[:, None]
    col_pos = (places % GRID_W).astype(jnp.float32)[:, None]
    index = jnp.arange(64, dtype=jnp.float32)[None, :]
    freq_row = jnp.exp(-(index - 8.0) / 28.0 * jnp.log(rope_theta))
    freq_col = jnp.exp(-(index - 36.0) / 28.0 * jnp.log(rope_theta))
    angle = jnp.where(
        index < 8.0, 0.0 * row_pos, jnp.where(index < 36.0, row_pos * freq_row, col_pos * freq_col)
    )
    cosine = jnp.cos(angle)[:, None, :]
    sine = jnp.sin(angle)[:, None, :]
    pairs = heads.reshape(row_count, HEADS, 64, 2)
    first = pairs[..., 0]
    second = pairs[..., 1]
    turned = jnp.stack([first * cosine - second * sine, first * sine + second * cosine], axis=-1)
    return turned.reshape(row_count, HEADS, HEAD_DIM)


def update(state_tuple, queries, pair_block):
    running_max, running_sum, running_acc = state_tuple
    key_block = pair_block[0]
    value_block = pair_block[1]
    scores = jnp.einsum("rhd,nhd->rhn", queries, key_block, preferred_element_type=jnp.float32)
    scores = scores / jnp.sqrt(jnp.float32(HEAD_DIM))
    new_max = jnp.maximum(running_max, jnp.max(scores, axis=-1))
    fade_out = jnp.exp(running_max - new_max)
    expo = jnp.exp(scores - new_max[..., None])
    new_sum = running_sum * fade_out + jnp.sum(expo, axis=-1)
    added = jnp.einsum(
        "rhn,nhd->rhd", expo.astype(jnp.bfloat16), value_block, preferred_element_type=jnp.float32
    )
    new_acc = running_acc * fade_out[..., None] + added
    return (new_max, new_sum, new_acc)


def regroup_swap(piece, bit_number):
    return from_partner(piece, "blk", bit_number)


def restore_swap(piece, bit_number):
    return from_partner(piece, "blk", bit_number)


def among_four(stacked, mover):
    index_here = lax.axis_index("blk")
    for bit_number in (0, 1):
        position = 1 - bit_number
        own_bit = index_here >> bit_number & 1
        kept_half = lax.dynamic_index_in_dim(stacked, own_bit, position, keepdims=False)
        sent_half = lax.dynamic_index_in_dim(stacked, 1 - own_bit, position, keepdims=False)
        received = mover(sent_half, bit_number)
        stacked = jnp.where(
            own_bit == 0,
            jnp.stack([kept_half, received], axis=position),
            jnp.stack([received, kept_half], axis=position),
        )
    return stacked


def move_upward(pair_block):
    return passed_along(pair_block, "blk", 4)


def move_downward(pair_block):
    return passed_along(pair_block, "blk", -4)


def per_device(txt_q, txt_k, txt_v, img_q, img_k, img_v, q_gain, k_gain, places):
    txt_count = txt_q.shape[0]
    img_count = img_q.shape[0]
    local_count = txt_count + img_count
    quarter = HEADS // 4
    queries = jnp.concatenate(
        [
            normed(txt_q, q_gain).astype(jnp.bfloat16),
            rotate(normed(img_q, q_gain), places).astype(jnp.bfloat16),
        ],
        axis=0,
    )
    keys_local = jnp.concatenate(
        [
            normed(txt_k, k_gain).astype(jnp.bfloat16),
            rotate(normed(img_k, k_gain), places).astype(jnp.bfloat16),
        ],
        axis=0,
    )
    values_local = jnp.concatenate([txt_v, img_v], axis=0).reshape(local_count, HEADS, HEAD_DIM)
    stacked = jnp.stack([queries, keys_local, values_local], axis=1).reshape(
        local_count, 3, 4, quarter, HEAD_DIM
    )
    stacked = jnp.transpose(stacked, (2, 0, 1, 3, 4)).reshape(
        2, 2, local_count, 3, quarter, HEAD_DIM
    )
    grouped = among_four(stacked, regroup_swap).reshape(4 * local_count, 3, quarter, HEAD_DIM)
    group_q = grouped[:, 0]
    own_pair = jnp.stack([grouped[:, 1], grouped[:, 2]], axis=0)
    group_rows = 4 * local_count
    blocks = lax.axis_size("blk") // 4
    soft_state = (
        jnp.full((group_rows, quarter), -jnp.inf, jnp.float32),
        jnp.zeros((group_rows, quarter), jnp.float32),
        jnp.zeros((group_rows, quarter, HEAD_DIM), jnp.float32),
    )
    soft_state = update(soft_state, group_q, own_pair)
    downward_turns = (blocks - 1) // 2

    def both_turn(turn, loop_state):
        upward, downward, inner = loop_state
        upward = move_upward(upward)
        downward = move_downward(downward)
        inner = update(inner, group_q, upward)
        inner = update(inner, group_q, downward)
        return (upward, downward, inner)

    upward, _, soft_state = lax.fori_loop(
        0, downward_turns, both_turn, (own_pair, own_pair, soft_state)
    )
    upward = move_upward(upward)
    soft_state = update(soft_state, group_q, upward)
    _, running_sum, running_acc = soft_state
    result = (running_acc / running_sum[..., None]).astype(jnp.bfloat16)
    result = result.reshape(2, 2, local_count, quarter, HEAD_DIM)
    returned = among_four(result, restore_swap).reshape(4, local_count, quarter, HEAD_DIM)
    returned = jnp.transpose(returned, (1, 0, 2, 3)).reshape(local_count, HEADS * HEAD_DIM)
    return (returned[:txt_count], returned[txt_count:])


ANY_SPEC = pl.BlockSpec(memory_space=pltpu.HBM)
SMEM_SPEC = pl.BlockSpec(memory_space=pltpu.SMEM)
VMEM_SPEC = pl.BlockSpec(memory_space=pltpu.VMEM)


def ring_next(plane):
    return ((plane & 1) << 1) | (1 - (plane >> 1))


def ring_back(plane):
    return ((1 - (plane & 1)) << 1) | (plane >> 1)


def ring_over(plane):
    return 3 - plane


def slots_of(plane):
    return (plane, ring_next(plane), ring_back(plane), ring_over(plane))


def unit_rows(x, gain):
    return x * lax.rsqrt(jnp.mean(x * x, axis=-1, keepdims=True) + 1e-06) * gain


def turn_tables(places_ref):
    count = places_ref.shape[1]
    spot = lax.broadcasted_iota(jnp.int32, (count, count), 0) == lax.broadcasted_iota(
        jnp.int32, (count, count), 1
    )
    patch = places_ref[...].astype(jnp.float32)
    patch = jnp.sum(jnp.where(spot, patch, 0.0), axis=1, keepdims=True)
    row_pos = jnp.floor(patch * (1.0 / GRID_W))
    col_pos = patch - row_pos * GRID_W
    lane = lax.broadcasted_iota(jnp.int32, (1, HEAD_DIM), 1)
    index = (lane >> 1).astype(jnp.float32)
    log_theta = jnp.float32(math.log(rope_theta))
    freq_row = jnp.exp(-(index - 8.0) / 28.0 * log_theta)
    freq_col = jnp.exp(-(index - 36.0) / 28.0 * log_theta)
    angle = jnp.where(
        index < 8.0, 0.0 * row_pos, jnp.where(index < 36.0, row_pos * freq_row, col_pos * freq_col)
    )
    even = (lane & 1) == 0
    sine = jnp.sin(angle)
    return jnp.cos(angle), jnp.where(even, -sine, sine), even


def turned(x, tables):
    cosine, sine, even = tables
    partner = jnp.where(even, pltpu.roll(x, HEAD_DIM - 1, 1), pltpu.roll(x, 1, 1))
    return x * cosine + partner * sine


def prepare(plane, tables, gain, txt_ref, img_ref, out_refs, lead):
    txt_count, width = txt_ref.shape
    share = width // len(out_refs)
    for part, out_ref in zip(slots_of(plane), out_refs):
        for off in range(0, share, HEAD_DIM):
            cols = pl.ds(pl.multiple_of(part * share + off, HEAD_DIM), HEAD_DIM)
            txt = unit_rows(txt_ref[:, cols].astype(jnp.float32), gain)
            img = turned(unit_rows(img_ref[:, cols].astype(jnp.float32), gain), tables)
            dest = slice(off, off + HEAD_DIM)
            out_ref[lead + (slice(0, txt_count), dest)] = txt.astype(jnp.bfloat16)
            out_ref[lead + (slice(txt_count, None), dest)] = img.astype(jnp.bfloat16)


def fetch(sources, targets, sems):
    copies = [
        pltpu.make_async_copy(src, dst, sems.at[i])
        for i, (src, dst) in enumerate(zip(sources, targets))
    ]
    for copy in copies:
        copy.start()
    return copies


def keys_kernel(plane_ref, places_hbm, gain_hbm, txt_k, img_k, txt_v, img_v, *refs):
    outs, (places_ref, gain_ref, txt_ref, img_ref, txt_val, img_val, sems) = refs[:4], refs[4:]
    copies = fetch(
        (places_hbm, gain_hbm, txt_k, img_k, txt_v, img_v),
        (places_ref, gain_ref, txt_ref, img_ref, txt_val, img_val),
        sems,
    )
    plane = plane_ref[0]
    copies[0].wait()
    tables = turn_tables(places_ref)
    for copy in copies[1:]:
        copy.wait()
    prepare(plane, tables, gain_ref[...], txt_ref, img_ref, outs, (0,))
    txt_count, width = txt_val.shape
    share = width // len(outs)
    for part, out_ref in zip(slots_of(plane), outs):
        cols = pl.ds(pl.multiple_of(part * share, HEAD_DIM), share)
        out_ref[1, :txt_count] = txt_val[:, cols]
        out_ref[1, txt_count:] = img_val[:, cols]


def queries_kernel(plane_ref, places_hbm, gain_hbm, txt_q, img_q, *refs):
    outs, (places_ref, gain_ref, txt_ref, img_ref, sems) = refs[:4], refs[4:]
    copies = fetch(
        (places_hbm, gain_hbm, txt_q, img_q), (places_ref, gain_ref, txt_ref, img_ref), sems
    )
    copies[0].wait()
    tables = turn_tables(places_ref)
    for copy in copies[1:]:
        copy.wait()
    prepare(plane_ref[0], tables, gain_ref[...], txt_ref, img_ref, outs, ())


def pack_kernel(*refs):
    pieces, out_ref = refs[:-1], refs[-1]
    start = 0
    for piece in pieces:
        stop = start + piece.shape[1]
        out_ref[:, start:stop] = piece[...]
        start = stop


def stage_kernel(*refs):
    pieces, (key_ref, value_ref) = refs[:-2], refs[-2:]
    start = 0
    for piece in pieces:
        stop = start + piece.shape[1]
        key_ref[start:stop] = piece[0]
        value_ref[start:stop] = piece[1]
        start = stop


def attend_kernel(*refs):
    count = (len(refs) - 2) // 2
    query_refs, key_ref, value_ref = refs[:count], refs[count], refs[count + 1]
    out_refs = refs[count + 2:]
    rows, share = query_refs[0].shape
    scale = 1.0 / math.sqrt(HEAD_DIM)
    for off in range(0, share, HEAD_DIM):
        cols = slice(off, off + HEAD_DIM)
        q = jnp.concatenate([ref[:, cols] for ref in query_refs], axis=0)
        s = lax.dot_general(
            q, key_ref[:, cols], (((1,), (1,)), ((), ())), preferred_element_type=jnp.float32
        )
        top = jnp.max(s, axis=-1, keepdims=True)
        expo = jnp.exp((s - top) * scale)
        total = jnp.sum(expo, axis=-1, keepdims=True)
        mixed = jnp.dot(
            expo.astype(jnp.bfloat16), value_ref[:, cols], preferred_element_type=jnp.float32
        )
        result = (mixed / total).astype(jnp.bfloat16)
        for i, ref in enumerate(out_refs):
            ref[:, cols] = result[i * rows:(i + 1) * rows]


def gather_kernel(plane_ref, *refs):
    pieces, (txt_ref, img_ref) = refs[:-2], refs[-2:]
    txt_count = txt_ref.shape[0]
    share = pieces[0].shape[1]
    for part, piece in zip(slots_of(plane_ref[0]), pieces):
        cols = pl.ds(pl.multiple_of(part * share, HEAD_DIM), share)
        txt_ref[:, cols] = piece[:txt_count]
        img_ref[:, cols] = piece[txt_count:]


def kernel_call(body, mib, outs, in_specs, scratch=()):
    def call(*args):
        return pl.pallas_call(
            body,
            out_shape=[jax.ShapeDtypeStruct(dims, jnp.bfloat16) for dims in outs],
            in_specs=in_specs,
            out_specs=[VMEM_SPEC] * len(outs),
            scratch_shapes=list(scratch),
            compiler_params=pltpu.CompilerParams(vmem_limit_bytes=mib << 20),
        )(*args)

    return call


def along_planes(block, move):
    count = lax.axis_size("blk")
    return lax.ppermute(block, "blk", [(i, move(i >> 2) << 2 | i & 3) for i in range(count)])


def in_plane(block, bits):
    count = lax.axis_size("blk")
    return lax.ppermute(block, "blk", [(i, i ^ bits) for i in range(count)])


def plane_body(txt_q, txt_k, txt_v, img_q, img_k, img_v, q_gain, k_gain, places):
    txt_count, width = txt_q.shape
    img_count = img_q.shape[0]
    rows = txt_count + img_count
    share = width // 4
    plane = (lax.axis_index("blk") >> 2).reshape(1)
    txt_q, txt_k, txt_v, img_q, img_k, img_v, q_gain, k_gain, spots = (
        pltpu.with_memory_space_constraint(x, pltpu.HBM)
        for x in (
            txt_q, txt_k, txt_v, img_q, img_k, img_v,
            q_gain.reshape(1, -1), k_gain.reshape(1, -1), places.reshape(1, -1),
        )
    )
    small = [pltpu.VMEM((1, img_count), jnp.int32), pltpu.VMEM((1, HEAD_DIM), jnp.float32)]
    pair = [pltpu.VMEM((txt_count, width), jnp.bfloat16), pltpu.VMEM((img_count, width), jnp.bfloat16)]
    own, kv_next, kv_back, kv_over = kernel_call(
        keys_kernel, 8, [(2, rows, share)] * 4, [SMEM_SPEC] + [ANY_SPEC] * 6,
        small + pair + pair + [pltpu.SemaphoreType.DMA((6,))],
    )(plane, spots, k_gain, txt_k, img_k, txt_v, img_v)
    q_own, q_next, q_back, q_over = kernel_call(
        queries_kernel, 8, [(rows, share)] * 4, [SMEM_SPEC] + [ANY_SPEC] * 4,
        small + pair + [pltpu.SemaphoreType.DMA((4,))],
    )(plane, spots, q_gain, txt_q, img_q)
    kv_next = along_planes(kv_next, ring_next)
    kv_back = along_planes(kv_back, ring_back)
    kv_over = along_planes(kv_over, ring_over)
    q_next = along_planes(q_next, ring_next)
    q_back = along_planes(q_back, ring_back)
    q_over = along_planes(q_over, ring_over)

    def pack(*pieces):
        return kernel_call(
            pack_kernel, 4, [(2, sum(p.shape[1] for p in pieces), share)],
            [VMEM_SPEC] * len(pieces),
        )(*pieces)[0]

    middle = pack(kv_next, kv_back)
    x_own = in_plane(own, 2)
    x_middle = in_plane(middle, 2)
    x_over = in_plane(kv_over, 2)
    first = pack(own, x_own, middle)
    second = pack(kv_over, x_middle)
    c_first = in_plane(first, 1)
    c_second = in_plane(second, 1)
    c_third = in_plane(x_over, 1)
    pieces = (first, c_first, second, c_second, x_over, c_third)
    keys, values = kernel_call(
        stage_kernel, 6, [(16 * rows, share)] * 2, [VMEM_SPEC] * len(pieces)
    )(*pieces)

    def attend(*queries):
        count = len(queries)
        return kernel_call(
            attend_kernel, 16, [(rows, share)] * count, [VMEM_SPEC] * (count + 2)
        )(*queries, keys, values)

    o_next, o_over = attend(q_next, q_over)
    (o_back,) = attend(q_back)
    (o_own,) = attend(q_own)
    o_next = along_planes(o_next, ring_back)
    o_over = along_planes(o_over, ring_over)
    o_back = along_planes(o_back, ring_next)
    return tuple(
        kernel_call(
            gather_kernel, 6, [(txt_count, width), (img_count, width)],
            [SMEM_SPEC] + [VMEM_SPEC] * 4,
        )(plane, o_own, o_next, o_back, o_over)
    )


def solution(mesh):
    placed = (
        P(("groups", "blk"), None),
        P(("groups", "blk"), None),
        P(("groups", "blk"), None),
        P(("groups", "blk"), None),
        P(("groups", "blk"), None),
        P(("groups", "blk"), None),
        P(),
        P(),
        P(("groups", "blk")),
    )
    specs = (P(("groups", "blk"), None), P(("groups", "blk"), None))

    def sharded(body):
        return jax.shard_map(
            body, mesh=mesh, in_specs=placed, out_specs=specs, check_vma=False
        )

    if mesh.shape["blk"] // 4 != 4:
        return sharded(per_device)
    return sharded(plane_body)
```

```python
import functools
import math
import jax
import jax.numpy as jnp
from jax import lax
from jax.experimental import pallas as pl
from jax.experimental.pallas import tpu as pltpu
from jax.sharding import PartitionSpec as P

HEADS = 12
HEAD_DIM = 128
GRID_W = 256


rope_theta = 10000.0


def from_partner(block, axis, apart):
    count = lax.axis_size(axis)
    route = []
    for low in range(count):
        high = low | 1 << apart
        if high != low and high < count:
            route += [(low, high), (high, low)]
    return lax.ppermute(block, axis, route)


def passed_along(block, axis, distance):
    devices = range(lax.axis_size(axis))
    route = [((i - distance) % len(devices), i) for i in devices]
    return lax.ppermute(block, axis, route)


def normed(values, gain):
    row_count = values.shape[0]
    heads = values.astype(jnp.float32).reshape(row_count, HEADS, HEAD_DIM)
    mean_sq = jnp.mean(heads * heads, axis=-1, keepdims=True)
    return heads * lax.rsqrt(mean_sq + 1e-06) * gain


def rotate(heads, places):
    row_count = heads.shape[0]
    row_pos = (places // GRID_W).astype(jnp.float32)[:, None]
    col_pos = (places % GRID_W).astype(jnp.float32)[:, None]
    index = jnp.arange(64, dtype=jnp.float32)[None, :]
    freq_row = jnp.exp(-(index - 8.0) / 28.0 * jnp.log(rope_theta))
    freq_col = jnp.exp(-(index - 36.0) / 28.0 * jnp.log(rope_theta))
    angle = jnp.where(
        index < 8.0, 0.0 * row_pos, jnp.where(index < 36.0, row_pos * freq_row, col_pos * freq_col)
    )
    cosine = jnp.cos(angle)[:, None, :]
    sine = jnp.sin(angle)[:, None, :]
    pairs = heads.reshape(row_count, HEADS, 64, 2)
    first = pairs[..., 0]
    second = pairs[..., 1]
    turned = jnp.stack([first * cosine - second * sine, first * sine + second * cosine], axis=-1)
    return turned.reshape(row_count, HEADS, HEAD_DIM)


def update(state_tuple, queries, pair_block):
    running_max, running_sum, running_acc = state_tuple
    key_block = pair_block[0]
    value_block = pair_block[1]
    scores = jnp.einsum("rhd,nhd->rhn", queries, key_block, preferred_element_type=jnp.float32)
    scores = scores / jnp.sqrt(jnp.float32(HEAD_DIM))
    new_max = jnp.maximum(running_max, jnp.max(scores, axis=-1))
    fade_out = jnp.exp(running_max - new_max)
    expo = jnp.exp(scores - new_max[..., None])
    new_sum = running_sum * fade_out + jnp.sum(expo, axis=-1)
    added = jnp.einsum(
        "rhn,nhd->rhd", expo.astype(jnp.bfloat16), value_block, preferred_element_type=jnp.float32
    )
    new_acc = running_acc * fade_out[..., None] + added
    return (new_max, new_sum, new_acc)


def regroup_swap(piece, bit_number):
    return from_partner(piece, "blk", bit_number)


def restore_swap(piece, bit_number):
    return from_partner(piece, "blk", bit_number)


def among_four(stacked, mover):
    index_here = lax.axis_index("blk")
    for bit_number in (0, 1):
        position = 1 - bit_number
        own_bit = index_here >> bit_number & 1
        kept_half = lax.dynamic_index_in_dim(stacked, own_bit, position, keepdims=False)
        sent_half = lax.dynamic_index_in_dim(stacked, 1 - own_bit, position, keepdims=False)
        received = mover(sent_half, bit_number)
        stacked = jnp.where(
            own_bit == 0,
            jnp.stack([kept_half, received], axis=position),
            jnp.stack([received, kept_half], axis=position),
        )
    return stacked


def move_upward(pair_block):
    return passed_along(pair_block, "blk", 4)


def move_downward(pair_block):
    return passed_along(pair_block, "blk", -4)


def per_device(txt_q, txt_k, txt_v, img_q, img_k, img_v, q_gain, k_gain, places):
    txt_count = txt_q.shape[0]
    img_count = img_q.shape[0]
    local_count = txt_count + img_count
    quarter = HEADS // 4
    queries = jnp.concatenate(
        [
            normed(txt_q, q_gain).astype(jnp.bfloat16),
            rotate(normed(img_q, q_gain), places).astype(jnp.bfloat16),
        ],
        axis=0,
    )
    keys_local = jnp.concatenate(
        [
            normed(txt_k, k_gain).astype(jnp.bfloat16),
            rotate(normed(img_k, k_gain), places).astype(jnp.bfloat16),
        ],
        axis=0,
    )
    values_local = jnp.concatenate([txt_v, img_v], axis=0).reshape(local_count, HEADS, HEAD_DIM)
    stacked = jnp.stack([queries, keys_local, values_local], axis=1).reshape(
        local_count, 3, 4, quarter, HEAD_DIM
    )
    stacked = jnp.transpose(stacked, (2, 0, 1, 3, 4)).reshape(
        2, 2, local_count, 3, quarter, HEAD_DIM
    )
    grouped = among_four(stacked, regroup_swap).reshape(4 * local_count, 3, quarter, HEAD_DIM)
    group_q = grouped[:, 0]
    own_pair = jnp.stack([grouped[:, 1], grouped[:, 2]], axis=0)
    group_rows = 4 * local_count
    blocks = lax.axis_size("blk") // 4
    soft_state = (
        jnp.full((group_rows, quarter), -jnp.inf, jnp.float32),
        jnp.zeros((group_rows, quarter), jnp.float32),
        jnp.zeros((group_rows, quarter, HEAD_DIM), jnp.float32),
    )
    soft_state = update(soft_state, group_q, own_pair)
    downward_turns = (blocks - 1) // 2

    def both_turn(turn, loop_state):
        upward, downward, inner = loop_state
        upward = move_upward(upward)
        downward = move_downward(downward)
        inner = update(inner, group_q, upward)
        inner = update(inner, group_q, downward)
        return (upward, downward, inner)

    upward, _, soft_state = lax.fori_loop(
        0, downward_turns, both_turn, (own_pair, own_pair, soft_state)
    )
    upward = move_upward(upward)
    soft_state = update(soft_state, group_q, upward)
    _, running_sum, running_acc = soft_state
    result = (running_acc / running_sum[..., None]).astype(jnp.bfloat16)
    result = result.reshape(2, 2, local_count, quarter, HEAD_DIM)
    returned = among_four(result, restore_swap).reshape(4, local_count, quarter, HEAD_DIM)
    returned = jnp.transpose(returned, (1, 0, 2, 3)).reshape(local_count, HEADS * HEAD_DIM)
    return (returned[:txt_count], returned[txt_count:])


ANY_SPEC = pl.BlockSpec(memory_space=pltpu.HBM)
SMEM_SPEC = pl.BlockSpec(memory_space=pltpu.SMEM)
VMEM_SPEC = pl.BlockSpec(memory_space=pltpu.VMEM)


def ring_next(plane):
    return ((plane & 1) << 1) | (1 - (plane >> 1))


def ring_back(plane):
    return ((1 - (plane & 1)) << 1) | (plane >> 1)


def ring_over(plane):
    return 3 - plane


def slots_of(plane):
    return (plane, ring_next(plane), ring_back(plane), ring_over(plane))


def unit_rows(x, gain):
    return x * lax.rsqrt(jnp.mean(x * x, axis=-1, keepdims=True) + 1e-06) * gain


def turn_tables(places_ref):
    count = places_ref.shape[1]
    spot = lax.broadcasted_iota(jnp.int32, (count, count), 0) == lax.broadcasted_iota(
        jnp.int32, (count, count), 1
    )
    patch = places_ref[...].astype(jnp.float32)
    patch = jnp.sum(jnp.where(spot, patch, 0.0), axis=1, keepdims=True)
    row_pos = jnp.floor(patch * (1.0 / GRID_W))
    col_pos = patch - row_pos * GRID_W
    lane = lax.broadcasted_iota(jnp.int32, (1, HEAD_DIM), 1)
    index = (lane >> 1).astype(jnp.float32)
    log_theta = jnp.float32(math.log(rope_theta))
    freq_row = jnp.exp(-(index - 8.0) / 28.0 * log_theta)
    freq_col = jnp.exp(-(index - 36.0) / 28.0 * log_theta)
    angle = jnp.where(
        index < 8.0, 0.0 * row_pos, jnp.where(index < 36.0, row_pos * freq_row, col_pos * freq_col)
    )
    even = (lane & 1) == 0
    sine = jnp.sin(angle)
    return jnp.cos(angle), jnp.where(even, -sine, sine), even


def turned(x, tables):
    cosine, sine, even = tables
    partner = jnp.where(even, pltpu.roll(x, HEAD_DIM - 1, 1), pltpu.roll(x, 1, 1))
    return x * cosine + partner * sine


def prepare(plane, tables, gain, txt_ref, img_ref, out_refs, lead):
    txt_count, width = txt_ref.shape
    share = width // len(out_refs)
    for part, out_ref in zip(slots_of(plane), out_refs):
        for off in range(0, share, HEAD_DIM):
            cols = pl.ds(pl.multiple_of(part * share + off, HEAD_DIM), HEAD_DIM)
            txt = unit_rows(txt_ref[:, cols].astype(jnp.float32), gain)
            img = turned(unit_rows(img_ref[:, cols].astype(jnp.float32), gain), tables)
            dest = slice(off, off + HEAD_DIM)
            out_ref[lead + (slice(0, txt_count), dest)] = txt.astype(jnp.bfloat16)
            out_ref[lead + (slice(txt_count, None), dest)] = img.astype(jnp.bfloat16)


def fetch(sources, targets, sems):
    copies = [
        pltpu.make_async_copy(src, dst, sems.at[i])
        for i, (src, dst) in enumerate(zip(sources, targets))
    ]
    for copy in copies:
        copy.start()
    return copies


def keys_kernel(plane_ref, places_hbm, gain_hbm, txt_k, img_k, txt_v, img_v, *refs):
    outs, (places_ref, gain_ref, txt_ref, img_ref, sems, value_sems) = refs[:4], refs[4:]
    copies = fetch(
        (places_hbm, gain_hbm, txt_k, img_k), (places_ref, gain_ref, txt_ref, img_ref), sems
    )
    plane = plane_ref[0]
    txt_count, width = txt_k.shape
    share = width // len(outs)
    sources, targets = [], []
    for part, out_ref in zip(slots_of(plane), outs):
        cols = pl.ds(pl.multiple_of(part * share, HEAD_DIM), share)
        sources += [txt_v.at[:, cols], img_v.at[:, cols]]
        targets += [
            out_ref.at[1, pl.ds(0, txt_count)],
            out_ref.at[1, pl.ds(txt_count, img_k.shape[0])],
        ]
    value_copies = fetch(sources, targets, value_sems)
    copies[0].wait()
    tables = turn_tables(places_ref)
    for copy in copies[1:]:
        copy.wait()
    prepare(plane, tables, gain_ref[...], txt_ref, img_ref, outs, (0,))
    for copy in value_copies:
        copy.wait()


def queries_kernel(plane_ref, places_hbm, gain_hbm, txt_q, img_q, *refs):
    outs, (places_ref, gain_ref, txt_ref, img_ref, sems) = refs[:4], refs[4:]
    copies = fetch(
        (places_hbm, gain_hbm, txt_q, img_q), (places_ref, gain_ref, txt_ref, img_ref), sems
    )
    copies[0].wait()
    tables = turn_tables(places_ref)
    for copy in copies[1:]:
        copy.wait()
    prepare(plane_ref[0], tables, gain_ref[...], txt_ref, img_ref, outs, ())


def pack_kernel(*refs):
    pieces, out_ref = refs[:-1], refs[-1]
    start = 0
    for piece in pieces:
        stop = start + piece.shape[1]
        out_ref[:, start:stop] = piece[...]
        start = stop


def stage_kernel(*refs):
    pieces, (key_ref, value_ref) = refs[:-2], refs[-2:]
    start = 0
    for piece in pieces:
        stop = start + piece.shape[1]
        key_ref[start:stop] = piece[0]
        value_ref[start:stop] = piece[1]
        start = stop


def head_columns(share):
    return [slice(off, off + HEAD_DIM) for off in range(0, share, HEAD_DIM)]


def stacked_rows(refs, index):
    return jnp.concatenate([ref[index] for ref in refs], axis=0)


def score(queries, keys):
    return lax.dot_general(
        queries, keys, (((1,), (1,)), ((), ())), preferred_element_type=jnp.float32
    )


EXPONENT_SCALE = math.log2(math.e) / math.sqrt(HEAD_DIM)


def partial_kernel(*refs):
    query_refs, (key_ref, value_ref, stat_ref, acc_ref) = refs[:-4], refs[-4:]
    heads = head_columns(key_ref.shape[1])
    scores = [score(stacked_rows(query_refs, (slice(None), c)), key_ref[:, c]) for c in heads]
    for s, cols in zip(scores, heads):
        top = jnp.max(s, axis=-1, keepdims=True)
        expo = jnp.exp2((s - top) * EXPONENT_SCALE)
        total = jnp.sum(expo, axis=-1, keepdims=True)
        acc_ref[:, cols] = jnp.dot(
            expo.astype(jnp.bfloat16), value_ref[:, cols], preferred_element_type=jnp.float32
        )
        flat = (s.shape[0], HEAD_DIM)
        stat_ref[0, :, cols] = jnp.broadcast_to(top, flat)
        stat_ref[1, :, cols] = jnp.broadcast_to(total, flat)


def finish_kernel(early, fresh, *refs):
    count = early + fresh
    query_refs, state_refs = refs[:count], refs[count:-4 - count]
    (key_ref, value_ref, left_ref, right_ref), out_refs = refs[-4 - count:-count], refs[-count:]
    rows, share = query_refs[0].shape
    heads = head_columns(share)
    edge = early * rows
    late, whole = [], []
    for c in heads:
        queries = stacked_rows(query_refs, (slice(None), c))
        late.append(score(queries, stacked_rows((left_ref, right_ref), (0, slice(None), c))))
        whole.append(score(queries[edge:], key_ref[:, c]))
    for s, first, cols in zip(late, whole, heads):
        values = stacked_rows((left_ref, right_ref), (1, slice(None), cols))
        results = []
        if early:
            stat_ref, acc_ref = state_refs
            early_top = stat_ref[0, :, cols]
            top = jnp.maximum(early_top, jnp.max(s[:edge], axis=-1, keepdims=True))
            fade = jnp.exp2((early_top - top) * EXPONENT_SCALE)
            expo = jnp.exp2((s[:edge] - top[:, :1]) * EXPONENT_SCALE)
            total = stat_ref[1, :, cols] * fade + jnp.sum(expo, axis=-1, keepdims=True)
            added = jnp.dot(expo.astype(jnp.bfloat16), values, preferred_element_type=jnp.float32)
            results.append((acc_ref[:, cols] * fade + added) / total)
        top = jnp.maximum(
            jnp.max(first, axis=-1, keepdims=True), jnp.max(s[edge:], axis=-1, keepdims=True)
        )
        expo = jnp.exp2((first - top) * EXPONENT_SCALE)
        more = jnp.exp2((s[edge:] - top) * EXPONENT_SCALE)
        total = jnp.sum(expo, axis=-1, keepdims=True) + jnp.sum(more, axis=-1, keepdims=True)
        mixed = jnp.dot(
            expo.astype(jnp.bfloat16), value_ref[:, cols], preferred_element_type=jnp.float32
        )
        mixed += jnp.dot(more.astype(jnp.bfloat16), values, preferred_element_type=jnp.float32)
        results.append(mixed / total)
        result = jnp.concatenate(results, axis=0).astype(jnp.bfloat16)
        for i, ref in enumerate(out_refs):
            ref[:, cols] = result[i * rows:(i + 1) * rows]


def gather_kernel(plane_ref, *refs):
    pieces, (txt_ref, img_ref) = refs[:-2], refs[-2:]
    txt_count = txt_ref.shape[0]
    share = pieces[0].shape[1]
    for part, piece in zip(slots_of(plane_ref[0]), pieces):
        cols = pl.ds(pl.multiple_of(part * share, HEAD_DIM), share)
        txt_ref[:, cols] = piece[:txt_count]
        img_ref[:, cols] = piece[txt_count:]


def kernel_call(body, mib, outs, in_specs, scratch=(), kind=jnp.bfloat16):
    def call(*args):
        return pl.pallas_call(
            body,
            out_shape=[jax.ShapeDtypeStruct(dims, kind) for dims in outs],
            in_specs=in_specs,
            out_specs=[VMEM_SPEC] * len(outs),
            scratch_shapes=list(scratch),
            compiler_params=pltpu.CompilerParams(vmem_limit_bytes=mib << 20),
        )(*args)

    return call


def along_planes(block, move):
    count = lax.axis_size("blk")
    return lax.ppermute(block, "blk", [(i, move(i >> 2) << 2 | i & 3) for i in range(count)])


def in_plane(block, bits):
    count = lax.axis_size("blk")
    return lax.ppermute(block, "blk", [(i, i ^ bits) for i in range(count)])


def plane_body(txt_q, txt_k, txt_v, img_q, img_k, img_v, q_gain, k_gain, places):
    txt_count, width = txt_q.shape
    img_count = img_q.shape[0]
    rows = txt_count + img_count
    share = width // 4
    plane = (lax.axis_index("blk") >> 2).reshape(1)
    txt_q, txt_k, txt_v, img_q, img_k, img_v, q_gain, k_gain, spots = (
        pltpu.with_memory_space_constraint(x, pltpu.HBM)
        for x in (
            txt_q, txt_k, txt_v, img_q, img_k, img_v,
            q_gain.reshape(1, -1), k_gain.reshape(1, -1), places.reshape(1, -1),
        )
    )
    small = [pltpu.VMEM((1, img_count), jnp.int32), pltpu.VMEM((1, HEAD_DIM), jnp.float32)]
    pair = [pltpu.VMEM((txt_count, width), jnp.bfloat16), pltpu.VMEM((img_count, width), jnp.bfloat16)]
    own, kv_next, kv_back, kv_over = kernel_call(
        keys_kernel, 8, [(2, rows, share)] * 4, [SMEM_SPEC] + [ANY_SPEC] * 6,
        small + pair + [pltpu.SemaphoreType.DMA((4,)), pltpu.SemaphoreType.DMA((8,))],
    )(plane, spots, k_gain, txt_k, img_k, txt_v, img_v)
    q_own, q_next, q_back, q_over = kernel_call(
        queries_kernel, 8, [(rows, share)] * 4, [SMEM_SPEC] + [ANY_SPEC] * 4,
        small + pair + [pltpu.SemaphoreType.DMA((4,))],
    )(plane, spots, q_gain, txt_q, img_q)
    kv_next = along_planes(kv_next, ring_next)
    kv_back = along_planes(kv_back, ring_back)
    kv_over = along_planes(kv_over, ring_over)
    q_next = along_planes(q_next, ring_next)
    q_back = along_planes(q_back, ring_back)
    q_over = along_planes(q_over, ring_over)

    def pack(*pieces):
        return kernel_call(
            pack_kernel, 4, [(2, sum(p.shape[1] for p in pieces), share)],
            [VMEM_SPEC] * len(pieces),
        )(*pieces)[0]

    x_own = in_plane(own, 2)
    x_back = in_plane(kv_back, 2)
    x_next = in_plane(kv_next, 2)
    x_over = in_plane(kv_over, 2)
    first = pack(own, kv_back, x_own, x_back)
    second = pack(kv_over, kv_next, x_next)
    c_first = in_plane(first, 1)
    c_second = in_plane(second, 1)
    c_over = in_plane(x_over, 1)
    keys, values = kernel_call(
        stage_kernel, 6, [(14 * rows, share)] * 2, [VMEM_SPEC] * 4
    )(first, c_first, second, c_second)

    def partial(*queries):
        size = len(queries) * rows
        return kernel_call(
            partial_kernel, 16, [(2, size, share), (size, share)],
            [VMEM_SPEC] * (len(queries) + 2), kind=jnp.float32,
        )(*queries, keys, values)

    def finish(early, fresh, states):
        count = len(early) + len(fresh)
        return kernel_call(
            functools.partial(finish_kernel, len(early), len(fresh)), 12,
            [(rows, share)] * count, [VMEM_SPEC] * (count + len(states) + 4),
        )(*early, *fresh, *states, keys, values, x_over, c_over)

    states = partial(q_next, q_back)
    o_next, o_back, o_over = finish((q_next, q_back), (q_over,), states)
    (o_own,) = finish((), (q_own,), ())
    o_next = along_planes(o_next, ring_back)
    o_over = along_planes(o_over, ring_over)
    o_back = along_planes(o_back, ring_next)
    return tuple(
        kernel_call(
            gather_kernel, 6, [(txt_count, width), (img_count, width)],
            [SMEM_SPEC] + [VMEM_SPEC] * 4,
        )(plane, o_own, o_next, o_back, o_over)
    )


def solution(mesh):
    placed = (
        P(("groups", "blk"), None),
        P(("groups", "blk"), None),
        P(("groups", "blk"), None),
        P(("groups", "blk"), None),
        P(("groups", "blk"), None),
        P(("groups", "blk"), None),
        P(),
        P(),
        P(("groups", "blk")),
    )
    specs = (P(("groups", "blk"), None), P(("groups", "blk"), None))

    def sharded(body):
        return jax.shard_map(
            body, mesh=mesh, in_specs=placed, out_specs=specs, check_vma=False
        )

    if mesh.shape["blk"] // 4 != 4:
        return sharded(per_device)
    return sharded(plane_body)
```

```python
import functools
import math
import jax
import jax.numpy as jnp
from jax import lax
from jax.experimental import pallas as pl
from jax.experimental.pallas import tpu as pltpu
from jax.sharding import PartitionSpec as P

HEADS = 12
HEAD_DIM = 128
GRID_W = 256


rope_theta = 10000.0


def from_partner(block, axis, apart):
    count = lax.axis_size(axis)
    route = []
    for low in range(count):
        high = low | 1 << apart
        if high != low and high < count:
            route += [(low, high), (high, low)]
    return lax.ppermute(block, axis, route)


def passed_along(block, axis, distance):
    devices = range(lax.axis_size(axis))
    route = [((i - distance) % len(devices), i) for i in devices]
    return lax.ppermute(block, axis, route)


def normed(values, gain):
    row_count = values.shape[0]
    heads = values.astype(jnp.float32).reshape(row_count, HEADS, HEAD_DIM)
    mean_sq = jnp.mean(heads * heads, axis=-1, keepdims=True)
    return heads * lax.rsqrt(mean_sq + 1e-06) * gain


def rotate(heads, places):
    row_count = heads.shape[0]
    row_pos = (places // GRID_W).astype(jnp.float32)[:, None]
    col_pos = (places % GRID_W).astype(jnp.float32)[:, None]
    index = jnp.arange(64, dtype=jnp.float32)[None, :]
    freq_row = jnp.exp(-(index - 8.0) / 28.0 * jnp.log(rope_theta))
    freq_col = jnp.exp(-(index - 36.0) / 28.0 * jnp.log(rope_theta))
    angle = jnp.where(
        index < 8.0, 0.0 * row_pos, jnp.where(index < 36.0, row_pos * freq_row, col_pos * freq_col)
    )
    cosine = jnp.cos(angle)[:, None, :]
    sine = jnp.sin(angle)[:, None, :]
    pairs = heads.reshape(row_count, HEADS, 64, 2)
    first = pairs[..., 0]
    second = pairs[..., 1]
    turned = jnp.stack([first * cosine - second * sine, first * sine + second * cosine], axis=-1)
    return turned.reshape(row_count, HEADS, HEAD_DIM)


def update(state_tuple, queries, pair_block):
    running_max, running_sum, running_acc = state_tuple
    key_block = pair_block[0]
    value_block = pair_block[1]
    scores = jnp.einsum("rhd,nhd->rhn", queries, key_block, preferred_element_type=jnp.float32)
    scores = scores / jnp.sqrt(jnp.float32(HEAD_DIM))
    new_max = jnp.maximum(running_max, jnp.max(scores, axis=-1))
    fade_out = jnp.exp(running_max - new_max)
    expo = jnp.exp(scores - new_max[..., None])
    new_sum = running_sum * fade_out + jnp.sum(expo, axis=-1)
    added = jnp.einsum(
        "rhn,nhd->rhd", expo.astype(jnp.bfloat16), value_block, preferred_element_type=jnp.float32
    )
    new_acc = running_acc * fade_out[..., None] + added
    return (new_max, new_sum, new_acc)


def regroup_swap(piece, bit_number):
    return from_partner(piece, "blk", bit_number)


def restore_swap(piece, bit_number):
    return from_partner(piece, "blk", bit_number)


def among_four(stacked, mover):
    index_here = lax.axis_index("blk")
    for bit_number in (0, 1):
        position = 1 - bit_number
        own_bit = index_here >> bit_number & 1
        kept_half = lax.dynamic_index_in_dim(stacked, own_bit, position, keepdims=False)
        sent_half = lax.dynamic_index_in_dim(stacked, 1 - own_bit, position, keepdims=False)
        received = mover(sent_half, bit_number)
        stacked = jnp.where(
            own_bit == 0,
            jnp.stack([kept_half, received], axis=position),
            jnp.stack([received, kept_half], axis=position),
        )
    return stacked


def move_upward(pair_block):
    return passed_along(pair_block, "blk", 4)


def move_downward(pair_block):
    return passed_along(pair_block, "blk", -4)


def per_device(txt_q, txt_k, txt_v, img_q, img_k, img_v, q_gain, k_gain, places):
    txt_count = txt_q.shape[0]
    img_count = img_q.shape[0]
    local_count = txt_count + img_count
    quarter = HEADS // 4
    queries = jnp.concatenate(
        [
            normed(txt_q, q_gain).astype(jnp.bfloat16),
            rotate(normed(img_q, q_gain), places).astype(jnp.bfloat16),
        ],
        axis=0,
    )
    keys_local = jnp.concatenate(
        [
            normed(txt_k, k_gain).astype(jnp.bfloat16),
            rotate(normed(img_k, k_gain), places).astype(jnp.bfloat16),
        ],
        axis=0,
    )
    values_local = jnp.concatenate([txt_v, img_v], axis=0).reshape(local_count, HEADS, HEAD_DIM)
    stacked = jnp.stack([queries, keys_local, values_local], axis=1).reshape(
        local_count, 3, 4, quarter, HEAD_DIM
    )
    stacked = jnp.transpose(stacked, (2, 0, 1, 3, 4)).reshape(
        2, 2, local_count, 3, quarter, HEAD_DIM
    )
    grouped = among_four(stacked, regroup_swap).reshape(4 * local_count, 3, quarter, HEAD_DIM)
    group_q = grouped[:, 0]
    own_pair = jnp.stack([grouped[:, 1], grouped[:, 2]], axis=0)
    group_rows = 4 * local_count
    blocks = lax.axis_size("blk") // 4
    soft_state = (
        jnp.full((group_rows, quarter), -jnp.inf, jnp.float32),
        jnp.zeros((group_rows, quarter), jnp.float32),
        jnp.zeros((group_rows, quarter, HEAD_DIM), jnp.float32),
    )
    soft_state = update(soft_state, group_q, own_pair)
    downward_turns = (blocks - 1) // 2

    def both_turn(turn, loop_state):
        upward, downward, inner = loop_state
        upward = move_upward(upward)
        downward = move_downward(downward)
        inner = update(inner, group_q, upward)
        inner = update(inner, group_q, downward)
        return (upward, downward, inner)

    upward, _, soft_state = lax.fori_loop(
        0, downward_turns, both_turn, (own_pair, own_pair, soft_state)
    )
    upward = move_upward(upward)
    soft_state = update(soft_state, group_q, upward)
    _, running_sum, running_acc = soft_state
    result = (running_acc / running_sum[..., None]).astype(jnp.bfloat16)
    result = result.reshape(2, 2, local_count, quarter, HEAD_DIM)
    returned = among_four(result, restore_swap).reshape(4, local_count, quarter, HEAD_DIM)
    returned = jnp.transpose(returned, (1, 0, 2, 3)).reshape(local_count, HEADS * HEAD_DIM)
    return (returned[:txt_count], returned[txt_count:])


ANY_SPEC = pl.BlockSpec(memory_space=pltpu.HBM)
SMEM_SPEC = pl.BlockSpec(memory_space=pltpu.SMEM)
VMEM_SPEC = pl.BlockSpec(memory_space=pltpu.VMEM)


def ring_next(plane):
    return ((plane & 1) << 1) | (1 - (plane >> 1))


def ring_back(plane):
    return ((1 - (plane & 1)) << 1) | (plane >> 1)


def ring_over(plane):
    return 3 - plane


def ring_slots(plane):
    return (plane, ring_next(plane), ring_back(plane), ring_over(plane))


def inverse_rms(x):
    return lax.rsqrt(jnp.mean(x * x, axis=-1, keepdims=True) + 1e-06)


def turn_tables(places_ref, gain):
    count = places_ref.shape[1]
    spot = lax.broadcasted_iota(jnp.int32, (count, count), 0) == lax.broadcasted_iota(
        jnp.int32, (count, count), 1
    )
    patch = places_ref[...].astype(jnp.float32)
    patch = jnp.sum(jnp.where(spot, patch, 0.0), axis=1, keepdims=True)
    row_pos = jnp.floor(patch * (1.0 / GRID_W))
    col_pos = patch - row_pos * GRID_W
    lane = lax.broadcasted_iota(jnp.int32, (1, HEAD_DIM), 1)
    index = (lane >> 1).astype(jnp.float32)
    log_theta = jnp.float32(math.log(rope_theta))
    freq_row = jnp.exp(-(index - 8.0) / 28.0 * log_theta)
    freq_col = jnp.exp(-(index - 36.0) / 28.0 * log_theta)
    angle = jnp.where(
        index < 8.0, 0.0 * row_pos, jnp.where(index < 36.0, row_pos * freq_row, col_pos * freq_col)
    )
    even = (lane & 1) == 0
    sine = jnp.sin(angle)
    turned_gain = jnp.where(even, pltpu.roll(gain, HEAD_DIM - 1, 1), pltpu.roll(gain, 1, 1))
    return jnp.cos(angle) * gain, jnp.where(even, -sine, sine) * turned_gain


def partner_matrix():
    row = lax.broadcasted_iota(jnp.int32, (HEAD_DIM, HEAD_DIM), 0)
    col = lax.broadcasted_iota(jnp.int32, (HEAD_DIM, HEAD_DIM), 1)
    return jnp.where(row == (col ^ 1), 1.0, 0.0).astype(jnp.bfloat16)


def prepare(slots, tables, gain, txt_ref, img_ref, out_refs, lead):
    gain_cosine, gain_sine = tables
    swap = partner_matrix()
    txt_count, width = txt_ref.shape
    share = width // len(out_refs)
    for part, out_ref in zip(slots, out_refs):
        for off in range(0, share, HEAD_DIM):
            cols = pl.ds(pl.multiple_of(part * share + off, HEAD_DIM), HEAD_DIM)
            dest = slice(off, off + HEAD_DIM)
            txt = txt_ref[:, cols].astype(jnp.float32)
            out_ref[lead + (slice(0, txt_count), dest)] = (
                txt * inverse_rms(txt) * gain
            ).astype(jnp.bfloat16)
            given = img_ref[:, cols]
            partner = jnp.dot(given, swap, preferred_element_type=jnp.float32)
            img = given.astype(jnp.float32)
            out_ref[lead + (slice(txt_count, None), dest)] = (
                (img * gain_cosine + partner * gain_sine) * inverse_rms(img)
            ).astype(jnp.bfloat16)


def fetch(sources, targets, sems):
    copies = [
        pltpu.make_async_copy(src, dst, sems.at[i])
        for i, (src, dst) in enumerate(zip(sources, targets))
    ]
    for copy in copies:
        copy.start()
    return copies


def keys_kernel(plane_ref, places_hbm, gain_hbm, txt_k, img_k, txt_v, img_v, *refs):
    outs, (places_ref, gain_ref, txt_ref, img_ref, sems, value_sems) = refs[:4], refs[4:]
    copies = fetch(
        (places_hbm, gain_hbm, txt_k, img_k), (places_ref, gain_ref, txt_ref, img_ref), sems
    )
    plane = plane_ref[0]
    txt_count, width = txt_k.shape
    share = width // len(outs)
    sources, targets = [], []
    for part, out_ref in zip(ring_slots(plane), outs):
        cols = pl.ds(pl.multiple_of(part * share, HEAD_DIM), share)
        sources += [txt_v.at[:, cols], img_v.at[:, cols]]
        targets += [
            out_ref.at[1, pl.ds(0, txt_count)],
            out_ref.at[1, pl.ds(txt_count, img_k.shape[0])],
        ]
    value_copies = fetch(sources, targets, value_sems)
    for copy in copies[:2]:
        copy.wait()
    tables = turn_tables(places_ref, gain_ref[...])
    for copy in copies[2:]:
        copy.wait()
    prepare(ring_slots(plane), tables, gain_ref[...], txt_ref, img_ref, outs, (0,))
    for copy in value_copies:
        copy.wait()


def queries_kernel(plane_ref, places_hbm, gain_hbm, txt_q, img_q, *refs):
    outs, (places_ref, gain_ref, txt_ref, img_ref, sems) = refs[:4], refs[4:]
    copies = fetch(
        (places_hbm, gain_hbm, txt_q, img_q), (places_ref, gain_ref, txt_ref, img_ref), sems
    )
    for copy in copies[:2]:
        copy.wait()
    tables = turn_tables(places_ref, gain_ref[...])
    for copy in copies[2:]:
        copy.wait()
    prepare(ring_slots(plane_ref[0]), tables, gain_ref[...], txt_ref, img_ref, outs, ())


def pack_kernel(*refs):
    pieces, out_ref = refs[:-1], refs[-1]
    start = 0
    for piece in pieces:
        stop = start + piece.shape[1]
        out_ref[:, start:stop] = piece[...]
        start = stop


def stage_kernel(*refs):
    pieces, (key_ref, value_ref) = refs[:-2], refs[-2:]
    start = 0
    for piece in pieces:
        stop = start + piece.shape[1]
        key_ref[start:stop] = piece[0]
        value_ref[start:stop] = piece[1]
        start = stop


def head_columns(share):
    return [slice(off, off + HEAD_DIM) for off in range(0, share, HEAD_DIM)]


def stacked_rows(refs, index):
    return jnp.concatenate([ref[index] for ref in refs], axis=0)


def score(queries, keys):
    return lax.dot_general(
        queries, keys, (((1,), (1,)), ((), ())), preferred_element_type=jnp.float32
    )


EXPONENT_SCALE = math.log2(math.e) / math.sqrt(HEAD_DIM)


def partial_kernel(*refs):
    query_refs, (key_ref, value_ref, stat_ref, acc_ref) = refs[:-4], refs[-4:]
    heads = head_columns(key_ref.shape[1])
    scores = [score(stacked_rows(query_refs, (slice(None), c)), key_ref[:, c]) for c in heads]
    for s, cols in zip(scores, heads):
        top = jnp.max(s, axis=-1, keepdims=True)
        expo = jnp.exp2((s - top) * EXPONENT_SCALE)
        total = jnp.sum(expo, axis=-1, keepdims=True)
        acc_ref[:, cols] = jnp.dot(
            expo.astype(jnp.bfloat16), value_ref[:, cols], preferred_element_type=jnp.float32
        )
        flat = (s.shape[0], HEAD_DIM)
        stat_ref[0, :, cols] = jnp.broadcast_to(top, flat)
        stat_ref[1, :, cols] = jnp.broadcast_to(total, flat)


def finish_kernel(groups, fresh, *refs):
    early = sum(groups)
    count, states = early + fresh, 2 * len(groups)
    query_refs, state_refs, refs = refs[:count], refs[count:count + states], refs[count + states:]
    (key_ref, value_ref, left_ref, right_ref), out_refs = refs[:4], refs[4:]
    rows, share = query_refs[0].shape
    heads = head_columns(share)
    edge = early * rows
    late, whole = [], []
    for c in heads:
        queries = stacked_rows(query_refs, (slice(None), c))
        late.append(score(queries, stacked_rows((left_ref, right_ref), (0, slice(None), c))))
        whole.append(score(queries[edge:], key_ref[:, c]) if fresh else None)
    for s, first, cols in zip(late, whole, heads):
        values = stacked_rows((left_ref, right_ref), (1, slice(None), cols))
        results = []
        if early:
            early_top = stacked_rows(state_refs[::2], (0, slice(None), cols))
            top = jnp.maximum(early_top, jnp.max(s[:edge], axis=-1, keepdims=True))
            fade = jnp.exp2((early_top - top) * EXPONENT_SCALE)
            expo = jnp.exp2((s[:edge] - top[:, :1]) * EXPONENT_SCALE)
            total = stacked_rows(state_refs[::2], (1, slice(None), cols)) * fade
            total += jnp.sum(expo, axis=-1, keepdims=True)
            added = jnp.dot(expo.astype(jnp.bfloat16), values, preferred_element_type=jnp.float32)
            results.append((stacked_rows(state_refs[1::2], (slice(None), cols)) * fade + added) / total)
        if fresh:
            top = jnp.maximum(
                jnp.max(first, axis=-1, keepdims=True), jnp.max(s[edge:], axis=-1, keepdims=True)
            )
            expo = jnp.exp2((first - top) * EXPONENT_SCALE)
            more = jnp.exp2((s[edge:] - top) * EXPONENT_SCALE)
            total = jnp.sum(expo, axis=-1, keepdims=True) + jnp.sum(more, axis=-1, keepdims=True)
            mixed = jnp.dot(
                expo.astype(jnp.bfloat16), value_ref[:, cols], preferred_element_type=jnp.float32
            )
            mixed += jnp.dot(more.astype(jnp.bfloat16), values, preferred_element_type=jnp.float32)
            results.append(mixed / total)
        result = jnp.concatenate(results, axis=0).astype(jnp.bfloat16)
        for i, ref in enumerate(out_refs):
            ref[:, cols] = result[i * rows:(i + 1) * rows]


def gather_kernel(plane_ref, *refs):
    pieces, (txt_ref, img_ref) = refs[:-2], refs[-2:]
    txt_count = txt_ref.shape[0]
    share = pieces[0].shape[1]
    for part, piece in zip(ring_slots(plane_ref[0]), pieces):
        cols = pl.ds(pl.multiple_of(part * share, HEAD_DIM), share)
        txt_ref[:, cols] = piece[:txt_count]
        img_ref[:, cols] = piece[txt_count:]


def kernel_call(body, mib, outs, in_specs, scratch=(), kind=jnp.bfloat16):
    def call(*args):
        return pl.pallas_call(
            body,
            out_shape=[jax.ShapeDtypeStruct(dims, kind) for dims in outs],
            in_specs=in_specs,
            out_specs=[VMEM_SPEC] * len(outs),
            scratch_shapes=list(scratch),
            compiler_params=pltpu.CompilerParams(vmem_limit_bytes=mib << 20),
        )(*args)

    return call


def along_planes(block, move):
    count = lax.axis_size("blk")
    return lax.ppermute(block, "blk", [(i, move(i >> 2) << 2 | i & 3) for i in range(count)])


def in_plane(block, bits):
    count = lax.axis_size("blk")
    return lax.ppermute(block, "blk", [(i, i ^ bits) for i in range(count)])


def plane_body(txt_q, txt_k, txt_v, img_q, img_k, img_v, q_gain, k_gain, places):
    txt_count, width = txt_q.shape
    img_count = img_q.shape[0]
    rows = txt_count + img_count
    share = width // 4
    plane = (lax.axis_index("blk") >> 2).reshape(1)
    txt_q, txt_k, txt_v, img_q, img_k, img_v, q_gain, k_gain, spots = (
        pltpu.with_memory_space_constraint(x, pltpu.HBM)
        for x in (
            txt_q, txt_k, txt_v, img_q, img_k, img_v,
            q_gain.reshape(1, -1), k_gain.reshape(1, -1), places.reshape(1, -1),
        )
    )
    small = [pltpu.VMEM((1, img_count), jnp.int32), pltpu.VMEM((1, HEAD_DIM), jnp.float32)]
    pair = [pltpu.VMEM((txt_count, width), jnp.bfloat16), pltpu.VMEM((img_count, width), jnp.bfloat16)]
    own, kv_next, kv_back, kv_over = kernel_call(
        keys_kernel, 8, [(2, rows, share)] * 4, [SMEM_SPEC] + [ANY_SPEC] * 6,
        small + pair + [pltpu.SemaphoreType.DMA((4,)), pltpu.SemaphoreType.DMA((8,))],
    )(plane, spots, k_gain, txt_k, img_k, txt_v, img_v)
    q_own, q_next, q_back, q_over = kernel_call(
        queries_kernel, 8, [(rows, share)] * 4, [SMEM_SPEC] + [ANY_SPEC] * 4,
        small + pair + [pltpu.SemaphoreType.DMA((4,))],
    )(plane, spots, q_gain, txt_q, img_q)
    kv_next = along_planes(kv_next, ring_next)
    kv_back = along_planes(kv_back, ring_back)
    kv_over = along_planes(kv_over, ring_over)
    q_next = along_planes(q_next, ring_next)
    q_back = along_planes(q_back, ring_back)
    q_over = along_planes(q_over, ring_over)

    def pack(*pieces):
        return kernel_call(
            pack_kernel, 4, [(2, sum(p.shape[1] for p in pieces), share)],
            [VMEM_SPEC] * len(pieces),
        )(*pieces)[0]

    x_own = in_plane(own, 2)
    x_back = in_plane(kv_back, 2)
    x_next = in_plane(kv_next, 2)
    x_over = in_plane(kv_over, 2)
    first = pack(own, kv_back, x_own, x_back)
    second = pack(kv_over, kv_next, x_next)
    c_first = in_plane(first, 1)
    c_second = in_plane(second, 1)
    c_over = in_plane(x_over, 1)
    keys, values = kernel_call(
        stage_kernel, 6, [(14 * rows, share)] * 2, [VMEM_SPEC] * 4
    )(first, c_first, second, c_second)

    def partial(*queries):
        size = len(queries) * rows
        return kernel_call(
            partial_kernel, 16, [(2, size, share), (size, share)],
            [VMEM_SPEC] * (len(queries) + 2), kind=jnp.float32,
        )(*queries, keys, values)

    def finish(groups, early, fresh, states):
        count = len(early) + len(fresh)
        return kernel_call(
            functools.partial(finish_kernel, groups, len(fresh)), 12,
            [(rows, share)] * count, [VMEM_SPEC] * (count + len(states) + 4),
        )(*early, *fresh, *states, keys, values, x_over, c_over)

    states = partial(q_next, q_over)
    o_next, o_over, o_back = finish((2,), (q_next, q_over), (q_back,), states)
    (o_own,) = finish((), (), (q_own,), ())
    o_next = along_planes(o_next, ring_back)
    o_over = along_planes(o_over, ring_over)
    o_back = along_planes(o_back, ring_next)
    return tuple(
        kernel_call(
            gather_kernel, 6, [(txt_count, width), (img_count, width)],
            [SMEM_SPEC] + [VMEM_SPEC] * 4,
        )(plane, o_own, o_next, o_back, o_over)
    )


def solution(mesh):
    placed = (
        P(("groups", "blk"), None),
        P(("groups", "blk"), None),
        P(("groups", "blk"), None),
        P(("groups", "blk"), None),
        P(("groups", "blk"), None),
        P(("groups", "blk"), None),
        P(),
        P(),
        P(("groups", "blk")),
    )
    specs = (P(("groups", "blk"), None), P(("groups", "blk"), None))

    def sharded(body):
        return jax.shard_map(
            body, mesh=mesh, in_specs=placed, out_specs=specs, check_vma=False
        )

    if mesh.shape["blk"] // 4 != 4:
        return sharded(per_device)
    return sharded(plane_body)
```
